32 devices in a mesh: dp: 2 (over x), slot: 4 (over y, core), hid: 4 (over z).
Axes of the slice: x: 2, y: 2, z: 4, core: 2. Of those that a mesh axis runs over, the one named last changes fastest.
Arguments:
- master_weights: float32 [8, 3, 768, 2048], P('slot', None, 'hid', 'dp'), may hold values from -0.125 to 0.125
- first_moment: float32 [8, 3, 768, 2048], P('slot', None, 'hid', 'dp'), may hold values from -6 to 6
- second_moment: float32 [8, 3, 768, 2048], P('slot', None, 'hid', 'dp'), may hold values from 1 to 100
- tokens_one: bfloat16 [2048, 2048], P('dp'), may hold values from -6 to 6
- grad_out: bfloat16 [2048, 2048], P('dp'), may hold values from -6 to 6
- route_one: int32 [2048, 2], P('dp'), may hold values from 0 to 7, all different within a row
- prob_one: float32 [2048, 2], P('dp'), may hold values from 0.05 to 0.6
- tokens_two: bfloat16 [2048, 2048], P('dp'), may hold values from -6 to 6
- route_two: int32 [2048, 2], P('dp'), may hold values from 0 to 7, all different within a row
- prob_two: float32 [2048, 2], P('dp'), may hold values from 0.05 to 0.6
- old_order: int32 [8], replicated, may hold values from 0 to 7, each once
- new_order: int32 [8], replicated, may hold values from 0 to 7, each once
Outputs:
- moved_master: float32 [8, 3, 768, 2048], P('slot', None, 'hid', 'dp')
- moved_first: float32 [8, 3, 768, 2048], P('slot', None, 'hid', 'dp')
- moved_second: float32 [8, 3, 768, 2048], P('slot', None, 'hid', 'dp')
- next_output: bfloat16 [2048, 2048], P('dp', ('slot', 'hid'))
The draws below stay inside these ranges and needn't reach their ends.
Inputs may be any that keep to these rules, and one draw needn't show every extreme that they name: `old_order`: lists each of the 8 experts once. `new_order`: lists each of the 8 experts once. `route_one`: each row names 2 different experts. `route_two`: each row names 2 different experts.
All inputs are finite; a program needn't handle non-finite values.
Results may differ from the reference program's by a relative error of at most 0.017.
Values may be sent and summed in bfloat16 or wider, within the bound.
A program may use at most 192 MiB of HBM per device.

```python
import math
import jax
import jax.numpy as jnp
from jax import lax

D = 2048
FF = 768
TOP = 2
EXPERTS = 8
TOKENS = 2048


def shard_levels(key, dims, cuts, smallest, high):
    gain = 1.0
    for dim, blocks in cuts:
        steps = jax.random.uniform(jax.random.fold_in(jax.random.fold_in(key, 6), dim), (blocks,), jnp.float32, smallest / len(cuts), high / len(cuts))
        gain = gain * jnp.repeat(jnp.exp(steps), dims[dim] // blocks).reshape((-1,) + (1,) * (len(dims) - 1 - dim))
    return gain


def choose_distinct(rng, rows, count, top, lift):
    order = jax.random.permutation(jax.random.fold_in(rng, 1), count)
    boost = order
    for power in range(3):
        boost = boost * boost // count
    boost = boost * lift // count
    lots = jax.random.randint(jax.random.fold_in(rng, 2), (rows, count), 0, 4096) + boost
    holders = jax.random.permutation(jax.random.fold_in(rng, 3), rows)[jnp.arange(count) % rows]
    lots = jnp.where(jnp.arange(rows)[:, None] == holders[None, :], 1 << 14, lots)
    priority = lots * count + jnp.arange(count)
    return lax.top_k(priority.astype(jnp.int32), top)[1].astype(jnp.int32)


def bell_draw(stream_key, dims, scale, limit, shards=(), held_as=jnp.bfloat16):
    drawn = scale * jax.random.normal(stream_key, dims, jnp.float32)
    if shards:
        drawn = drawn * shard_levels(stream_key, dims, shards, -0.22, 0.18)
    return jnp.clip(drawn, -limit, limit).astype(held_as)


def setup_inputs(seed: int = 0) -> dict:
    keys = jax.random.split(jax.random.key(seed), 13)
    return {
        "master_weights": bell_draw(keys[0], (EXPERTS, 3, FF, D), D ** -0.5, 0.125, ((0, 4), (2, 4), (3, 2)), jnp.float32),
        "first_moment": bell_draw(keys[1], (EXPERTS, 3, FF, D), 1.0, 6.0, ((0, 4), (2, 4), (3, 2)), jnp.float32),
        "second_moment": jnp.clip(jnp.exp(math.log(100.0) - 4.6051702 * jax.random.uniform(keys[2], (EXPERTS, 3, FF, D), jnp.float32) ** shard_levels(keys[2], (EXPERTS, 3, FF, D), ((0, 4), (2, 4), (3, 2)), -0.2, 0.2)), 1.0, 100.0),
        "tokens_one": bell_draw(keys[3], (TOKENS, D), 1.0, 6.0, ((0, 2),)),
        "grad_out": bell_draw(keys[4], (TOKENS, D), 1.0, 6.0, ((0, 2),)),
        "route_one": choose_distinct(keys[5], TOKENS, EXPERTS, TOP, 4096),
        "prob_one": jnp.clip(0.05 + 0.55 * jax.random.uniform(keys[6], (TOKENS, TOP), jnp.float32) ** shard_levels(keys[6], (TOKENS, TOP), ((0, 2),), -0.2, 0.2), 0.05, 0.6),
        "tokens_two": bell_draw(keys[7], (TOKENS, D), 1.0, 6.0, ((0, 2),)),
        "route_two": choose_distinct(keys[8], TOKENS, EXPERTS, TOP, 4096),
        "prob_two": jnp.clip(0.05 + 0.55 * jax.random.uniform(keys[9], (TOKENS, TOP), jnp.float32) ** shard_levels(keys[9], (TOKENS, TOP), ((0, 2),), -0.2, 0.2), 0.05, 0.6),
        "old_order": jax.random.permutation(keys[10], EXPERTS).astype(jnp.int32),
        "new_order": jax.random.permutation(keys[11], EXPERTS).astype(jnp.int32),
    }


learn_rate = 0.001
beta_one = 0.9
beta_two = 0.95
epsilon = 1e-08
decay_rate = 0.1

def rows_by(left, right):
    return lax.dot_general(left, right, (((1,), (1,)), ((), ())), preferred_element_type=jnp.float32)

def cols_by(left, right):
    return lax.dot_general(left, right, (((0,), (0,)), ((), ())), preferred_element_type=jnp.float32)

def expert_grads(tokens, grad_out, scaling, weights):
    gate_proj = rows_by(tokens, weights[0])
    up_proj = rows_by(tokens, weights[1])
    logistic = jax.nn.sigmoid(gate_proj)
    swish_gate = gate_proj * logistic
    activated = (swish_gate * up_proj).astype(jnp.bfloat16)
    scaled_grad = (scaling[:, None] * grad_out.astype(jnp.float32)).astype(jnp.bfloat16)
    d_down = cols_by(activated, scaled_grad)
    d_activated = rows_by(scaled_grad, weights[2])
    d_gate = (d_activated * up_proj * logistic * (1.0 + gate_proj * (1.0 - logistic))).astype(jnp.bfloat16)
    d_up = (d_activated * swish_gate).astype(jnp.bfloat16)
    return jnp.stack([cols_by(d_gate, tokens), cols_by(d_up, tokens), d_down])

def expert_out(tokens, scaling, weights):
    gate_proj = rows_by(tokens, weights[0])
    up_proj = rows_by(tokens, weights[1])
    mixed = (scaling[:, None] * gate_proj * jax.nn.sigmoid(gate_proj) * up_proj).astype(jnp.bfloat16)
    return jnp.dot(mixed, weights[2], preferred_element_type=jnp.float32)

def adamw_update(master, moment_a, moment_b, grad_sum):
    new_a = beta_one * moment_a + (1.0 - beta_one) * grad_sum
    new_b = beta_two * moment_b + (1.0 - beta_two) * grad_sum * grad_sum
    fixed_a = new_a / (1.0 - beta_one ** 10)
    fixed_b = new_b / (1.0 - beta_two ** 10)
    new_master = master - learn_rate * (fixed_a / (jnp.sqrt(fixed_b) + epsilon) + decay_rate * master)
    return (new_master, new_a, new_b)

def coefficient(routes, probs, expert):
    return lax.optimization_barrier(jnp.sum(jnp.where(routes == expert, probs, 0.0), axis=1))

def reference(master_weights, first_moment, second_moment, tokens_one, grad_out, route_one, prob_one, tokens_two, route_two, prob_two, old_order, new_order):
    weights = master_weights.astype(jnp.bfloat16)
    gradients = []
    for position in range(EXPERTS):
        scaling = coefficient(route_one, prob_one, old_order[position])
        gradients.append(expert_grads(tokens_one, grad_out, scaling, weights[position]))
    gradients = jnp.stack(gradients)
    new_master, new_a, new_b = adamw_update(master_weights, first_moment, second_moment, gradients)
    positions = jnp.arange(EXPERTS, dtype=jnp.int32)
    source = lax.optimization_barrier(jnp.sum(jnp.where(old_order[None, :] == new_order[:, None], positions[None, :], 0), axis=1)).astype(jnp.int32)
    moved_master = jnp.take(new_master, source, axis=0)
    moved_first = jnp.take(new_a, source, axis=0)
    moved_second = jnp.take(new_b, source, axis=0)
    next_weights = moved_master.astype(jnp.bfloat16)
    combined = jnp.zeros((TOKENS, D), jnp.float32)
    for position in range(EXPERTS):
        scaling = coefficient(route_two, prob_two, new_order[position])
        combined = combined + expert_out(tokens_two, scaling, next_weights[position])
    return (moved_master, moved_first, moved_second, combined.astype(jnp.bfloat16))
```

```python
import jax
import jax.numpy as jnp
from jax import lax
from jax.sharding import PartitionSpec as P


learn_rate = 0.001
beta_one = 0.9
beta_two = 0.95
epsilon = 1e-08
decay_rate = 0.1


def rows_by(left, right):
    return lax.dot_general(
        left, right, (((1,), (1,)), ((), ())), preferred_element_type=jnp.float32
    )


def cols_by(left, right):
    return lax.dot_general(
        left, right, (((0,), (0,)), ((), ())), preferred_element_type=jnp.float32
    )


def adamw_update(master, moment_a, moment_b, grad_sum):
    new_a = beta_one * moment_a + (1.0 - beta_one) * grad_sum
    new_b = beta_two * moment_b + (1.0 - beta_two) * grad_sum * grad_sum
    fixed_a = new_a / (1.0 - beta_one**10)
    fixed_b = new_b / (1.0 - beta_two**10)
    new_master = master - learn_rate * (
        fixed_a / (jnp.sqrt(fixed_b) + epsilon) + decay_rate * master
    )
    return (new_master, new_a, new_b)


def coefficients(routes, probs, expert_ids):
    matches = routes[:, :, None] == expert_ids[None, None, :]
    return jnp.sum(jnp.where(matches, probs[:, :, None], 0.0), axis=1)


def flip(value, axis, bit, size):
    return lax.ppermute(value, axis, [(i, i ^ bit) for i in range(size)])


def pick(options, index):
    chosen = options[0]
    for place in range(1, len(options)):
        chosen = jnp.where(index == place, options[place], chosen)
    return chosen


def make_body(dp_size, slot_size, hid_size):
    def to_parts(own):
        if dp_size == 2:
            return [own, flip(own, "dp", 1, 2)]
        return [lax.all_gather(own, "dp", axis=own.ndim - 1, tiled=True)]

    def width_parts(tokens):
        if dp_size == 2:
            half = tokens.shape[1] // 2
            me = lax.axis_index("dp")
            return [
                lax.dynamic_slice_in_dim(tokens, me * half, half, 1),
                lax.dynamic_slice_in_dim(tokens, (1 - me) * half, half, 1),
            ]
        return [tokens]

    def project(token_parts, weight_parts):
        total = rows_by(token_parts[0], weight_parts[0])
        for left, right in zip(token_parts[1:], weight_parts[1:]):
            total = total + rows_by(left, right)
        return total

    def owned_grad(left, token_parts):
        if dp_size == 2:
            sent = cols_by(left, token_parts[1]).astype(jnp.bfloat16)
            came = flip(sent, "dp", 1, 2)
            return cols_by(left, token_parts[0]) + came.astype(jnp.float32)
        whole = cols_by(left, token_parts[0]).astype(jnp.bfloat16)
        return lax.psum_scatter(whole, "dp", scatter_dimension=1, tiled=True).astype(
            jnp.float32
        )

    def body(
        master_weights,
        first_moment,
        second_moment,
        tokens_one,
        grad_out,
        route_one,
        prob_one,
        tokens_two,
        route_two,
        prob_two,
        old_order,
        new_order,
    ):
        count, kinds, hidden, width = master_weights.shape
        slot_index = lax.axis_index("slot")
        offset = slot_index * count
        held_ids = lax.dynamic_slice_in_dim(old_order, offset, count)
        positions = jnp.arange(old_order.shape[0], dtype=jnp.int32)
        source = jnp.sum(
            jnp.where(old_order[None, :] == new_order[:, None], positions[None, :], 0),
            axis=1,
        )
        pair_start = (slot_index // 2) * 2 * count
        wanted = lax.dynamic_slice_in_dim(source, offset, count)
        their_wanted = lax.dynamic_slice_in_dim(source, (slot_index ^ 2) * count, count)

        def place_of(position):
            local = position - pair_start
            inside = (local >= 0) & (local < 2 * count)
            mine = local - (slot_index % 2) * count
            other = local - (1 - slot_index % 2) * count
            is_mine = (mine >= 0) & (mine < count)
            return jnp.where(inside, jnp.where(is_mine, mine, count + other), 2 * count)

        my_places = [place_of(wanted[i]) for i in range(count)]
        their_places = [place_of(their_wanted[i]) for i in range(count)]

        def move(value):
            swapped = flip(value, "slot", 1, slot_size)
            near = [value[i] for i in range(count)] + [swapped[i] for i in range(count)]
            sent = jnp.stack([pick(near, place) for place in their_places])
            came = flip(sent, "slot", 2, slot_size)
            return [pick(near + [came[i]], my_places[i]) for i in range(count)]

        kind_weights = [
            master_weights[:, kind].reshape(count * hidden, width).astype(jnp.bfloat16)
            for kind in range(kinds)
        ]
        gate_w = to_parts(kind_weights[0])
        up_w = to_parts(kind_weights[1])
        down_w = to_parts(kind_weights[2])

        moved_old = [
            move(state.astype(jnp.bfloat16))
            for state in (master_weights, first_moment, second_moment)
        ]

        spread = lambda scaling: jnp.repeat(scaling, hidden, axis=1)
        scale_one = spread(coefficients(route_one, prob_one, held_ids))
        scale_two = spread(coefficients(route_two, prob_two, held_ids))

        token_parts = width_parts(tokens_one)
        grad_parts = width_parts(grad_out)
        gate_proj = project(token_parts, gate_w)
        up_proj = project(token_parts, up_w)
        logistic = jax.nn.sigmoid(gate_proj)
        swish_gate = gate_proj * logistic
        activated = (scale_one * swish_gate * up_proj).astype(jnp.bfloat16)
        gate_proj, up_proj, activated = lax.optimization_barrier(
            (gate_proj, up_proj, activated)
        )
        logistic = jax.nn.sigmoid(gate_proj)
        swish_gate = gate_proj * logistic
        grad_down = owned_grad(activated, grad_parts)
        d_activated = scale_one * project(grad_parts, down_w)
        d_gate = (
            d_activated * up_proj * logistic * (1.0 + gate_proj * (1.0 - logistic))
        ).astype(jnp.bfloat16)
        grad_gate = owned_grad(d_gate, token_parts)
        d_up = (d_activated * swish_gate).astype(jnp.bfloat16)
        grad_up = owned_grad(d_up, token_parts)

        def updated(kind, grad):
            shaped = grad.reshape(count, hidden, width)
            fresh = adamw_update(
                master_weights[:, kind], first_moment[:, kind], second_moment[:, kind], shaped
            )[0]
            return fresh.reshape(count * hidden, width).astype(jnp.bfloat16)

        next_down = to_parts(updated(2, grad_down))
        next_gate = to_parts(updated(0, grad_gate))
        next_up = to_parts(updated(1, grad_up))

        grads = jnp.stack(
            [
                grad.reshape(count, hidden, width).astype(jnp.bfloat16)
                for grad in (grad_gate, grad_up, grad_down)
            ],
            axis=1,
        )
        moved_grads = move(grads)
        results = [
            adamw_update(
                moved_old[0][i].astype(jnp.float32),
                moved_old[1][i].astype(jnp.float32),
                moved_old[2][i].astype(jnp.float32),
                moved_grads[i].astype(jnp.float32),
            )
            for i in range(count)
        ]
        moved_states = [jnp.stack([result[j] for result in results]) for j in range(3)]

        two_parts = width_parts(tokens_two)
        gate_two = project(two_parts, next_gate)
        up_two = project(two_parts, next_up)
        mixed = (scale_two * gate_two * jax.nn.sigmoid(gate_two) * up_two).astype(jnp.bfloat16)

        pair, member = slot_index // 2, slot_index % 2
        full_width = tokens_one.shape[1]
        half = full_width // 2
        quarter = half // 2
        if dp_size == 2:
            same = pair == lax.axis_index("dp")
            down_keep = jnp.where(same, next_down[0], next_down[1])
            down_send = jnp.where(same, next_down[1], next_down[0])
        else:
            down_keep = lax.dynamic_slice_in_dim(next_down[0], pair * half, half, 1)
            down_send = lax.dynamic_slice_in_dim(next_down[0], (1 - pair) * half, half, 1)

        def pair_sum(block):
            sent = lax.dynamic_slice_in_dim(block, (1 - member) * quarter, quarter, 1)
            kept = lax.dynamic_slice_in_dim(block, member * quarter, quarter, 1)
            away = jnp.dot(mixed, sent, preferred_element_type=jnp.float32)
            came = flip(away.astype(jnp.bfloat16), "slot", 1, slot_size)
            stay = jnp.dot(mixed, kept, preferred_element_type=jnp.float32)
            return stay + came.astype(jnp.float32)

        away = pair_sum(down_send).astype(jnp.bfloat16)
        came = flip(away, "slot", 2, slot_size)
        total = pair_sum(down_keep) + came.astype(jnp.float32)
        hid_index = lax.axis_index("hid")
        piece = quarter // hid_size
        rounded = total.astype(jnp.bfloat16)
        out = lax.dynamic_slice_in_dim(total, hid_index * piece, piece, 1)
        for shift in range(1, hid_size):
            target = (hid_index + shift) % hid_size
            block = lax.dynamic_slice_in_dim(rounded, target * piece, piece, 1)
            ring = [(i, (i + shift) % hid_size) for i in range(hid_size)]
            out = out + lax.ppermute(block, "hid", ring).astype(jnp.float32)
        return (*moved_states, out.astype(jnp.bfloat16))

    return body


def solution(mesh):
    sizes = mesh.shape
    states = P("slot", None, "hid", "dp")
    rows = P("dp", None)
    in_specs = (states,) * 3 + (rows,) * 7 + (P(), P())
    out_specs = (states,) * 3 + (P("dp", ("slot", "hid")),)
    body = make_body(sizes["dp"], sizes["slot"], sizes["hid"])

    return jax.shard_map(
        body, mesh=mesh, in_specs=in_specs, out_specs=out_specs, check_vma=False
    )
```
